512 devices in a mesh: occi: 16 (over y_lo, z), occj: 32 (over y_hi, x, core).
Axes of the slice: x: 4, y: 8 (y_hi: 4, y_lo: 2; y = y_hi * 2 + y_lo), z: 8, core: 2. Of those that a mesh axis runs over, the one named last changes fastest.
Arguments:
- amplitudes: float32 [32, 32, 512, 512], P('occi', 'occj'), may hold values from -6 to 6
- vectors: bfloat16 [3, 512, 512], P(None, 'occj'), may hold values from -0.25 to 0.25
- occupied_fock_block: bfloat16 [32, 32], replicated, may hold values from -1 to 1
- occ_energy: float32 [32], replicated, may hold values from -3 to -0.3
- vir_energy: float32 [512], replicated, may hold values from 0.2 to 4
Outputs:
- updated: float32 [32, 32, 512, 512], P('occi', 'occj')
The draws below stay inside these ranges and needn't reach their ends.
All inputs are finite; a program needn't handle non-finite values.
Results may differ from the reference program's by a relative error of at most 0.0028.
Values may be sent and summed in bfloat16 or wider, within the bound.
A program may use at most 64 MiB of HBM per device.

```python
import jax
import jax.numpy as jnp
from jax import lax

V = 512
NCHOL = 3
ITERS = 2
NO = 32


def levels(own_key, extent, cuts, low, largest):
    gain = 1.0
    for dim, parts in cuts:
        steps = jax.random.uniform(jax.random.fold_in(jax.random.fold_in(own_key, 6), dim), (parts,), jnp.float32, low / len(cuts), largest / len(cuts))
        gain = gain * jnp.repeat(jnp.exp(steps), extent[dim] // parts).reshape((-1,) + (1,) * (len(extent) - 1 - dim))
    return gain


def gaussian(rng, shape, deviation, most, split=(), kind=jnp.bfloat16):
    loudness = levels(rng, shape, split, -0.22, 0.18) if split else 1.0
    values = jax.random.normal(rng, shape, jnp.float32) * deviation * loudness
    return jnp.minimum(jnp.maximum(values, -most), most).astype(kind)


def setup_inputs(seed: int = 0) -> dict:
    streams_of = jax.random.split(jax.random.key(seed), 6)
    amplitudes = gaussian(streams_of[0], (NO, NO, V, V), 1.0, 6.0, ((0, 16), (1, 32)), jnp.float32)
    vectors = gaussian(streams_of[1], (NCHOL, V, V), V ** -0.5, 0.25, ((1, 32),))
    occupied_fock_block = gaussian(streams_of[2], (NO, NO), NO ** -0.5, 1.0)
    occ_energy = jnp.clip(jax.random.uniform(streams_of[3], (NO,), jnp.float32, -3.0, -0.3), -3.0, -0.3)
    vir_energy = jnp.clip(jax.random.uniform(streams_of[4], (V,), jnp.float32, 0.2, 4.0), 0.2, 4.0)
    return {"amplitudes": amplitudes, "vectors": vectors, "occupied_fock_block": occupied_fock_block, "occ_energy": occ_energy, "vir_energy": vir_energy}


def round_trip(values):
    return lax.optimization_barrier(values.astype(jnp.bfloat16)).astype(jnp.float32)


def half_residual(reduced_precision_copy, occupied_fock_block, vectors):
    vec_full = vectors.astype(jnp.float32)
    rounded_wide = reduced_precision_copy.astype(jnp.float32)
    flattened_row_list = rounded_wide.reshape(reduced_precision_copy.shape[0], -1)
    fock_wide = occupied_fock_block.astype(jnp.float32)

    def one_row(position):
        pair_rows = rounded_wide[position]
        running = jnp.zeros(pair_rows.shape, jnp.float32)
        for vector_id in range(NCHOL):
            single = vec_full[vector_id]
            inner = jnp.einsum("jcd,bd->jcb", pair_rows, single, precision=lax.Precision.HIGHEST)
            inner = round_trip(inner)
            running = running + jnp.einsum("ac,jcb->jab", single, inner, precision=lax.Precision.HIGHEST)
        ladder = round_trip(running)
        column = lax.dynamic_slice_in_dim(fock_wide, position, 1, 1)
        mixed = -jnp.dot(column[:, 0][None, :], flattened_row_list, precision=lax.Precision.HIGHEST).reshape(pair_rows.shape)
        return (ladder + mixed).astype(jnp.bfloat16)

    return lax.map(one_row, jnp.arange(NO, dtype=jnp.int32))


def reference(amplitudes, vectors, occupied_fock_block, occ_energy, vir_energy):
    denominator = ((occ_energy[:, None, None, None] + occ_energy[None, :, None, None])
                   - vir_energy[None, None, :, None]) - vir_energy[None, None, None, :]
    current = amplitudes
    for iteration in range(ITERS):
        reduced_precision_copy = current.astype(jnp.bfloat16)
        half = half_residual(reduced_precision_copy, occupied_fock_block, vectors).astype(jnp.float32)
        residual = half + jnp.transpose(half, (1, 0, 3, 2))
        current = current + residual / denominator
    return current
```

```python
import functools

import jax
import jax.numpy as jnp
from jax import lax
from jax.experimental import pallas as pl
from jax.experimental.pallas import tpu as pltpu
from jax.sharding import PartitionSpec as P

MESH = pl.DeviceIdType.MESH
NI, NJ = 16, 32
B = 128
PAIRS = ((0, 1), (0, 2), (0, 3), (1, 2), (1, 3), (2, 3))
PLACES = PAIRS + ((0, 0), (2, 2)) + tuple((b, a) for a, b in PAIRS) + ((1, 1), (3, 3))


def kernel(
    amp_ref, vec_ref, fock_ref, occ_ref, vir_ref, out_ref,
    t0, tb, vg, kron, inner, blk, tsl, lblk, lsl, mix, hs, hm, us, uh, ms, hm2, ws, wh, lu,
    amp_sem, vs_sem, vr_sem, xs_sem, xr_sem, ts_sem, tr_sem, ls_sem, lr_sem,
    hs_sem, hr_sem, us_sem, ur_sem, ms_sem, mr_sem, ws_sem, wr_sem,
):
    p = lax.axis_index("occi")
    q = lax.axis_index("occj")
    ylo, z = p // 8, p % 8
    r, core = q // 2, q % 2
    yhi, x = r // 4, r % 4
    flip = (p + 8) % NI
    mirror = (p + 8 * (1 - z // 6)) % NI

    load = pltpu.make_async_copy(amp_ref, t0, amp_sem)
    load.start()

    barrier = pltpu.get_barrier_semaphore()

    def greet(dev):
        pl.semaphore_signal(barrier, inc=1, device_id=dev, device_id_type=MESH)

    def greet_column(t, c):
        greet(((p + t) % NI, q))
        return c

    def greet_row(t, c):
        greet((p, (q + t) % NJ))
        greet((flip, (q + t) % NJ))
        return c

    lax.fori_loop(1, NI, greet_column, 0)
    lax.fori_loop(1, NJ, greet_row, 0)

    rows = lax.broadcasted_iota(jnp.int32, (512, NJ), 0) // 16
    cols = lax.broadcasted_iota(jnp.int32, (512, NJ), 1)
    spread = (rows == cols).astype(jnp.float32).astype(jnp.bfloat16)
    wide = lax.dot_general(
        fock_ref[...], spread, (((0,), (1,)), ((), ())), preferred_element_type=jnp.float32
    ).astype(jnp.bfloat16)
    tall = jnp.dot(spread, wide, preferred_element_type=jnp.float32)
    same = (
        lax.broadcasted_iota(jnp.int32, (512, 512), 0) % 16
        == lax.broadcasted_iota(jnp.int32, (512, 512), 1) % 16
    )
    kron[...] = jnp.where(same, -tall, 0.0).astype(jnp.bfloat16)

    load.wait()
    for s in range(2):
        for place, (ka, kb) in enumerate(PLACES):
            part = t0[s, ka * B:(ka + 1) * B, kb * B:(kb + 1) * B].astype(jnp.bfloat16)
            blk[place, s] = part
            tb[s, ka * B:(ka + 1) * B, kb * B:(kb + 1) * B] = part

    pl.semaphore_wait(barrier, NI - 1 + 2 * (NJ - 1))

    vg[:, r, core] = vec_ref[...]
    sign = 2 * ylo - 1
    y = 2 * yhi + ylo

    def send_vec(ty, tx):
        ny = (y + sign * ty + 8) % 8
        nx = (x + tx) % 4
        pltpu.make_async_remote_copy(
            vec_ref, vg.at[:, r, core], vs_sem, vr_sem,
            device_id=((ny % 2) * 8 + z, ((ny // 2) * 4 + nx) * 2 + core), device_id_type=MESH,
        ).start()

    def send_vec_far(t, c):
        send_vec(1 + t // 4, t % 4)
        return c

    def send_vec_near(t, c):
        send_vec(0, t)
        return c

    lax.fori_loop(0, 12, send_vec_far, 0)
    lax.fori_loop(1, 4, send_vec_near, 0)

    def send_block(src, dst, send, recv, k):
        @pl.when(k != p)
        def _():
            pltpu.make_async_remote_copy(
                src, dst, send, recv, device_id=(k, q), device_id_type=MESH
            ).start()

        @pl.when(k == p)
        def _():
            pltpu.make_async_copy(src, dst, recv).start()

    def send_t(t, c):
        zi = t // 2
        dz = ((zi + 1) // 2) * (2 * (zi % 2) - 1)
        k = ((ylo + t % 2) % 2) * 8 + (z + dz + 8) % 8
        send_block(blk.at[k], tsl.at[pl.ds(2 * p, 2)], ts_sem, tr_sem, k)
        return c

    lax.fori_loop(0, NI, send_t, 0)

    most = vg.at[:, pl.ds(0, 15), 0]
    pltpu.make_async_copy(most, most, vr_sem).wait()
    other = 2 * r + 1 - core
    swap = pltpu.make_async_remote_copy(
        vg.at[:, :, core], vg.at[:, :, core], xs_sem, xr_sem,
        device_id=(p, other), device_id_type=MESH,
    )
    swap.start()
    swap.wait_send()
    pltpu.make_async_copy(vg.at[:, :, 0], vg.at[:, :, 0], xr_sem).wait()

    def ladder(source, store):
        def first(s, c):
            for h in range(2):
                piece = source[s, h * 256:(h + 1) * 256, :]
                for l in range(3):
                    inner[s, l, h * 256:(h + 1) * 256, :] = lax.dot_general(
                        piece, vg[l].reshape(512, 512), (((1,), (1,)), ((), ())),
                        preferred_element_type=jnp.float32,
                    ).astype(jnp.bfloat16)
            return c

        def second(s, c):
            for h in range(2):
                total = None
                for l in range(3):
                    term = jnp.dot(
                        vg[l, h * 8:(h + 1) * 8].reshape(256, 512), inner[s, l],
                        preferred_element_type=jnp.float32,
                    )
                    total = term if total is None else total + term
                store(s, h, total)
            return c

        lax.fori_loop(0, 2, first, 0)
        lax.fori_loop(0, 2, second, 0)

    def store_blocks(s, h, total):
        for place, (ka, kb) in enumerate(PLACES):
            if ka // 2 == h:
                lblk[place, s] = total[(ka % 2) * B:(ka % 2 + 1) * B, kb * B:(kb + 1) * B].astype(jnp.bfloat16)

    ladder(tb, store_blocks)

    def send_l(t, c):
        k = (p + 2 * NI - r - t) % NI
        send_block(lblk.at[k], lsl.at[pl.ds(2 * p, 2)], ls_sem, lr_sem.at[p], k)
        return c

    lax.fori_loop(0, NI, send_l, 0)

    def mixing(source):
        def group(g, c):
            lines = pl.ds(pl.multiple_of(g * 16, 16), 16)
            got = jnp.dot(
                kron[...], source[:, lines, :].reshape(512, B), preferred_element_type=jnp.float32
            )
            mix[:, lines, :] = got.reshape(NJ, 16, B)
            return c

        lax.fori_loop(0, B // 16, group, 0)

    pltpu.make_async_copy(tsl, tsl, tr_sem).wait()
    mixing(tsl)

    def send_mirror(src, dst, send, recv, i):
        alone = (mirror == p) & (i == q)

        @pl.when(jnp.logical_not(alone))
        def _():
            pltpu.make_async_remote_copy(
                src, dst, send, recv, device_id=(mirror, i), device_id_type=MESH
            ).start()

        @pl.when(alone)
        def _():
            pltpu.make_async_copy(src, dst, recv).start()

    def halves(t, c):
        k = (p + r + t) % NI
        pltpu.make_async_copy(lblk.at[0], lsl.at[pl.ds(2 * k, 2)], lr_sem.at[k]).wait()
        for s in range(2):
            i = 2 * k + s
            hs[i] = (mix[i] + lsl[i].astype(jnp.float32)).astype(jnp.bfloat16)
            send_mirror(hs.at[i], hm.at[q], hs_sem, hr_sem.at[q], i)
        return c

    lax.fori_loop(0, NI, halves, 0)

    va = jnp.zeros((1, B), jnp.float32)
    vb = jnp.zeros((1, B), jnp.float32)
    for place, (ka, kb) in enumerate(PLACES):
        here = p == place
        va = jnp.where(here, vir_ref[ka:ka + 1, :], va)
        vb = jnp.where(here, vir_ref[kb:kb + 1, :], vb)
    va_block = jnp.transpose(jnp.broadcast_to(va, (B, B)))
    occ_j = occ_ref[q]

    def updates(t, c):
        k = (r + 2 * NI - mirror - t) % NI
        for s in range(2):
            i = 2 * k + s
            pltpu.make_async_copy(hs.at[0], hm.at[i], hr_sem.at[i]).wait()
            residual = hs[i].astype(jnp.float32) + jnp.transpose(hm[i].astype(jnp.float32))
            denominator = ((occ_ref[i] + occ_j) - va_block) - vb
            us[i] = (residual / denominator).astype(jnp.bfloat16)
        send_block(us.at[pl.ds(2 * k, 2)], uh.at[p], us_sem, ur_sem, k)
        return c

    lax.fori_loop(0, NI, updates, 0)

    mixing(us)

    def send_mix(t, c):
        k = (r + t) % NI
        for s in range(2):
            i = 2 * k + s
            ms[i] = mix[i].astype(jnp.bfloat16)
            send_mirror(ms.at[i], hm2.at[q], ms_sem, mr_sem.at[q], i)
        return c

    lax.fori_loop(0, NI, send_mix, 0)

    def sums(t, c):
        k = (r + NI - t) % NI
        for s in range(2):
            i = 2 * k + s
            pltpu.make_async_copy(ms.at[0], hm2.at[i], mr_sem.at[i]).wait()
            ws[i] = (mix[i] + jnp.transpose(hm2[i].astype(jnp.float32))).astype(jnp.bfloat16)
        send_block(ws.at[pl.ds(2 * k, 2)], wh.at[p], ws_sem, wr_sem, k)
        return c

    lax.fori_loop(0, NI, sums, 0)

    pltpu.make_async_copy(uh, uh, ur_sem).wait()
    for s in range(2):
        for place, (ka, kb) in enumerate(PLACES):
            tb[s, ka * B:(ka + 1) * B, kb * B:(kb + 1) * B] = uh[place, s]

    def store_plain(s, h, total):
        lu[s, h * 256:(h + 1) * 256, :] = total

    ladder(tb, store_plain)

    pltpu.make_async_copy(wh, wh, wr_sem).wait()
    for ka in range(4):
        va_block = jnp.transpose(jnp.broadcast_to(vir_ref[ka:ka + 1, :], (B, B)))
        for kb in range(4):
            place = PLACES.index((ka, kb))
            at = (slice(ka * B, (ka + 1) * B), slice(kb * B, (kb + 1) * B))
            for s in range(2):
                denominator = ((occ_ref[2 * p + s] + occ_j) - va_block) - vir_ref[kb:kb + 1, :]
                residual = 2.0 * lu[(s,) + at] + wh[place, s].astype(jnp.float32)
                out_ref[(s,) + at] = (
                    t0[(s,) + at] + 2.0 * uh[place, s].astype(jnp.float32) + residual / denominator
                )

    pltpu.make_async_copy(most, most, vs_sem).wait()
    rest = pl.ds(0, NI - 1)
    pltpu.make_async_copy(blk.at[rest], blk.at[rest], ts_sem).wait()
    pltpu.make_async_copy(lblk.at[rest], lblk.at[rest], ls_sem).wait()
    pltpu.make_async_copy(uh.at[rest], uh.at[rest], us_sem).wait()
    pltpu.make_async_copy(wh.at[rest], wh.at[rest], ws_sem).wait()
    alone = mirror == p

    @pl.when(alone)
    def _():
        left = pl.ds(0, NJ - 1)
        pltpu.make_async_copy(hs.at[left], hs.at[left], hs_sem).wait()
        pltpu.make_async_copy(ms.at[left], ms.at[left], ms_sem).wait()

    @pl.when(jnp.logical_not(alone))
    def _():
        pltpu.make_async_copy(hs, hs, hs_sem).wait()
        pltpu.make_async_copy(ms, ms, ms_sem).wait()


def local(amplitudes, vectors, occupied_fock_block, occ_energy, vir_energy):
    bf, f32 = jnp.bfloat16, jnp.float32
    dma = pltpu.SemaphoreType.DMA
    vmem = pl.BlockSpec(memory_space=pltpu.VMEM)
    out = pl.pallas_call(
        kernel,
        out_shape=jax.ShapeDtypeStruct((2, 512, 512), f32),
        in_specs=[
            pl.BlockSpec(memory_space=pl.ANY), vmem, vmem,
            pl.BlockSpec(memory_space=pltpu.SMEM), vmem,
        ],
        out_specs=vmem,
        scratch_shapes=[
            pltpu.VMEM((2, 512, 512), f32),
            pltpu.VMEM((2, 512, 512), bf),
            pltpu.VMEM((3, 16, 2, 16, 512), bf),
            pltpu.VMEM((512, 512), bf),
            pltpu.VMEM((2, 3, 512, 512), bf),
            pltpu.VMEM((NI, 2, B, B), bf),
            pltpu.VMEM((NJ, B, B), bf),
            pltpu.VMEM((NI, 2, B, B), bf),
            pltpu.VMEM((NJ, B, B), bf),
            pltpu.VMEM((NJ, B, B), f32),
            pltpu.VMEM((NJ, B, B), bf),
            pltpu.VMEM((NJ, B, B), bf),
            pltpu.VMEM((NJ, B, B), bf),
            pltpu.VMEM((NI, 2, B, B), bf),
            pltpu.VMEM((NJ, B, B), bf),
            pltpu.VMEM((NJ, B, B), bf),
            pltpu.VMEM((NJ, B, B), bf),
            pltpu.VMEM((NI, 2, B, B), bf),
            pltpu.VMEM((2, 512, 512), f32),
            dma, dma, dma, dma, dma, dma, dma,
            dma, dma((NI,)), dma, dma((NJ,)),
            dma, dma, dma, dma((NJ,)), dma, dma,
        ],
        compiler_params=pltpu.CompilerParams(
            collective_id=0, has_side_effects=True, vmem_limit_bytes=60 * 1024 * 1024
        ),
        name="doubles",
    )(
        amplitudes.reshape(2, 512, 512), vectors, occupied_fock_block, occ_energy,
        vir_energy.reshape(4, B),
    )
    return out.reshape(2, 1, 512, 512)


def solution(mesh):
    return jax.shard_map(
        local,
        mesh=mesh,
        in_specs=(P("occi", "occj", None, None), P(None, "occj", None), P(), P(), P()),
        out_specs=P("occi", "occj", None, None),
        check_vma=False,
    )
```

```python
import functools

import jax
import jax.numpy as jnp
from jax import lax
from jax.experimental import pallas as pl
from jax.experimental.pallas import tpu as pltpu
from jax.sharding import PartitionSpec as P

MESH = pl.DeviceIdType.MESH
NI, NJ = 16, 32
B = 128
PAIRS = ((0, 1), (0, 2), (0, 3), (1, 2), (1, 3), (2, 3))
PLACES = PAIRS + ((0, 0), (2, 2)) + tuple((b, a) for a, b in PAIRS) + ((1, 1), (3, 3))


def kernel(
    amp_ref, vec_ref, fock_ref, occ_ref, vir_ref, out_ref,
    t0, tb, tfl, vg, kron, inner, blk, tsl, lblk, lsl, mix, hs, hst, hm, us, uh, ms, hm2, ws, wh, lu,
    amp_sem, vs_sem, vr_sem, xs_sem, xr_sem, ts_sem, tr_sem, tfs_sem, tfr_sem, tgs_sem, tgr_sem, ls_sem, lr_sem,
    hs_sem, hr_sem, us_sem, ur_sem, ms_sem, mr_sem, ws_sem, wr_sem,
):
    p = lax.axis_index("occi")
    q = lax.axis_index("occj")
    ylo, z = p // 8, p % 8
    r, core = q // 2, q % 2
    yhi, x = r // 4, r % 4
    y = 2 * yhi + ylo
    other = 2 * r + 1 - core
    flip = (p + 8) % NI
    ours, theirs = 8 * ylo, 8 * (1 - ylo)
    mirror = (p + 8 * (1 - z // 6)) % NI

    load = pltpu.make_async_copy(amp_ref, t0, amp_sem)
    load.start()

    barrier = pltpu.get_barrier_semaphore()

    def greet(dev):
        pl.semaphore_signal(barrier, inc=1, device_id=dev, device_id_type=MESH)

    def greet_column(t, c):
        greet(((p + t) % NI, q))
        return c

    def at_y(ny, nx):
        return ((ny % 2) * 8 + z, ((ny // 2) * 4 + nx) * 2 + core)

    def greet_mirror(i, c):
        @pl.when(jnp.logical_not((mirror == p) & (i == q)))
        def _():
            greet((mirror, i))

        return c

    def greet_vec_near(t, c):
        greet(at_y(y, (x + t) % 4))
        return c

    def greet_vec_far(t, c):
        d = 1 + t // 4
        up = (d + y) % 2
        greet(at_y((y - d * up + d * (1 - up) + 8) % 8, (x + t) % 4))
        return c

    greet((p, other))
    lax.fori_loop(1, NI, greet_column, 0)
    lax.fori_loop(1, 4, greet_vec_near, 0)
    lax.fori_loop(0, 12, greet_vec_far, 0)
    lax.fori_loop(0, NJ, greet_mirror, 0)

    rows = lax.broadcasted_iota(jnp.int32, (512, NJ), 0) // 16
    cols = lax.broadcasted_iota(jnp.int32, (512, NJ), 1)
    spread = (rows == cols).astype(jnp.float32).astype(jnp.bfloat16)
    wide = lax.dot_general(
        fock_ref[...], spread, (((0,), (1,)), ((), ())), preferred_element_type=jnp.float32
    ).astype(jnp.bfloat16)
    tall = jnp.dot(spread, wide, preferred_element_type=jnp.float32)
    same = (
        lax.broadcasted_iota(jnp.int32, (512, 512), 0) % 16
        == lax.broadcasted_iota(jnp.int32, (512, 512), 1) % 16
    )
    kron[...] = jnp.where(same, -tall, 0.0).astype(jnp.bfloat16)

    load.wait()
    for s in range(2):
        for place, (ka, kb) in enumerate(PLACES):
            part = t0[s, ka * B:(ka + 1) * B, kb * B:(kb + 1) * B].astype(jnp.bfloat16)
            blk[place, s] = part
            tb[s, ka * B:(ka + 1) * B, kb * B:(kb + 1) * B] = part

    pl.semaphore_wait(barrier, 1 + NI - 1 + 15 + NJ - z // 6)

    vg[:, r, core] = vec_ref[...]
    sign = 2 * ylo - 1

    def send_vec(ty, tx):
        pltpu.make_async_remote_copy(
            vec_ref, vg.at[:, r, core], vs_sem, vr_sem,
            device_id=at_y((y + sign * ty + 8) % 8, (x + tx) % 4), device_id_type=MESH,
        ).start()

    def send_vec_far(t, c):
        send_vec(1 + t // 4, t % 4)
        return c

    def send_vec_near(t, c):
        send_vec(0, t)
        return c

    lax.fori_loop(0, 12, send_vec_far, 0)
    lax.fori_loop(1, 4, send_vec_near, 0)

    def send_block(src, dst, send, recv, k):
        @pl.when(k != p)
        def _():
            pltpu.make_async_remote_copy(
                src, dst, send, recv, device_id=(k, q), device_id_type=MESH
            ).start()

        @pl.when(k == p)
        def _():
            pltpu.make_async_copy(src, dst, recv).start()

    def cross_t(t, c):
        place = theirs + around(t)
        pltpu.make_async_remote_copy(
            blk.at[place], tfl.at[place], tfs_sem, tfr_sem.at[place - theirs],
            device_id=(flip, q), device_id_type=MESH,
        ).start()
        return c

    def around(t):
        return (z + ((t + 1) // 2) * (2 * (t % 2) - 1) + 8) % 8

    def send_t(t, c):
        k = ours + around(t)
        send_block(blk.at[k], tsl.at[pl.ds(2 * p, 2)], ts_sem, tr_sem, k)
        return c

    def pass_t(t, c):
        zk = around(t)
        pltpu.make_async_copy(blk.at[0], tfl.at[ours + zk], tfr_sem.at[zk]).wait()
        send_block(tfl.at[ours + zk], tsl.at[pl.ds(2 * flip, 2)], ts_sem, tr_sem, ours + zk)
        return c

    lax.fori_loop(0, 8, cross_t, 0)
    lax.fori_loop(0, 8, send_t, 0)
    lax.fori_loop(0, 8, pass_t, 0)

    most = vg.at[:, pl.ds(0, 15), 0]
    pltpu.make_async_copy(most, most, vr_sem).wait()
    pltpu.make_async_remote_copy(
        blk.at[pl.ds(ours, 8)], tfl.at[pl.ds(ours, 8)], tgs_sem, tgr_sem,
        device_id=(flip, q), device_id_type=MESH,
    ).start()
    swap = pltpu.make_async_remote_copy(
        vg.at[:, :, core], vg.at[:, :, core], xs_sem, xr_sem,
        device_id=(p, other), device_id_type=MESH,
    )
    swap.start()
    swap.wait_send()
    pltpu.make_async_copy(vg.at[:, :, 0], vg.at[:, :, 0], xr_sem).wait()

    def inner_half(s, c):
        for h in range(2):
            piece = tb[s, h * 256:(h + 1) * 256, :]
            for l in range(3):
                inner[s, l, h * 256:(h + 1) * 256, :] = lax.dot_general(
                    piece, vg[l].reshape(512, 512), (((1,), (1,)), ((), ())),
                    preferred_element_type=jnp.float32,
                ).astype(jnp.bfloat16)
        return c

    def outer(s, first, last, left, right):
        total = None
        for l in range(3):
            term = jnp.dot(
                vg[l, first * 4:last * 4].reshape((last - first) * B, 512),
                inner[s, l, :, left * B:right * B], preferred_element_type=jnp.float32,
            )
            total = term if total is None else total + term
        return total

    def ladder_blocks(turn):
        lax.fori_loop(0, 2, inner_half, 0)
        for plane, parts in enumerate((((0, 1, 0, 4), (1, 3, 2, 4)), ((3, 4, 0, 4), (1, 3, 0, 2)))):
            def one_pair(s, c, parts=parts, plane=plane):
                for first, last, left, right in parts:
                    total = outer(s, first, last, left, right)
                    for ka in range(first, last):
                        for kb in range(left, right):
                            zk = PLACES.index((ka, kb)) - 8 * plane
                            lblk[turn, zk, s] = total[
                                (ka - first) * B:(ka - first + 1) * B, (kb - left) * B:(kb - left + 1) * B
                            ].astype(jnp.bfloat16)
                return c

            @pl.when(ylo == plane)
            def _():
                lax.fori_loop(0, 2, one_pair, 0)

        origin = (p, flip)[turn]

        def send_l(t, c):
            zk = (z + 3 * NI - r - t) % 8
            send_block(
                lblk.at[turn, zk], lsl.at[pl.ds(2 * origin, 2)], ls_sem, lr_sem.at[origin], ours + zk
            )
            return c

        lax.fori_loop(0, 8, send_l, 0)

    ladder_blocks(0)

    def mixing(source):
        def group(g, c):
            lines = [pl.ds(pl.multiple_of(g * 32 + 16 * h, 16), 16) for h in range(2)]
            pieces = [source[:, at, :].reshape(512, B) for at in lines]
            got = jnp.dot(
                kron[...], jnp.concatenate(pieces, axis=1), preferred_element_type=jnp.float32
            )
            for h in range(2):
                mix[:, lines[h], :] = got[:, h * B:(h + 1) * B].reshape(NJ, 16, B)
            return c

        lax.fori_loop(0, B // 32, group, 0)

    pltpu.make_async_copy(tsl, tsl, tr_sem).wait()
    mixing(tsl)

    half_places = pl.ds(0, 8)
    pltpu.make_async_copy(blk.at[half_places], blk.at[half_places], tgr_sem).wait()
    for s in range(2):
        for place, (ka, kb) in enumerate(PLACES):
            tb[s, ka * B:(ka + 1) * B, kb * B:(kb + 1) * B] = tfl[place, s]
    ladder_blocks(1)

    def send_mirror(src, dst, send, recv, i):
        alone = (mirror == p) & (i == q)

        @pl.when(jnp.logical_not(alone))
        def _():
            pltpu.make_async_remote_copy(
                src, dst, send, recv, device_id=(mirror, i), device_id_type=MESH
            ).start()

        @pl.when(alone)
        def _():
            pltpu.make_async_copy(src, dst, recv).start()

    def halves(t, c):
        k = ((ylo + t // 8) % 2) * 8 + (z + r + t) % 8
        pltpu.make_async_copy(lblk.at[0, 0], lsl.at[pl.ds(2 * k, 2)], lr_sem.at[k]).wait()
        for s in range(2):
            i = 2 * k + s
            half = (mix[i] + lsl[i].astype(jnp.float32)).astype(jnp.bfloat16).astype(jnp.float32)
            hst[i] = jnp.transpose(half).astype(jnp.bfloat16)
            send_mirror(hst.at[i], hm.at[q], hs_sem, hr_sem.at[q], i)
            hs[i] = half.astype(jnp.bfloat16)
        return c

    lax.fori_loop(0, NI, halves, 0)

    va = jnp.zeros((1, B), jnp.float32)
    vb = jnp.zeros((1, B), jnp.float32)
    for place, (ka, kb) in enumerate(PLACES):
        here = p == place
        va = jnp.where(here, vir_ref[ka:ka + 1, :], va)
        vb = jnp.where(here, vir_ref[kb:kb + 1, :], vb)
    va_block = jnp.transpose(jnp.broadcast_to(va, (B, B)))
    occ_j = occ_ref[q]

    def updates(t, c):
        k = ((r // 8 + t) % 2) * 8 + (r + 2 * NI - z - t // 2) % 8
        for s in range(2):
            i = 2 * k + s
            pltpu.make_async_copy(hs.at[0], hm.at[i], hr_sem.at[i]).wait()
            residual = hs[i].astype(jnp.float32) + hm[i].astype(jnp.float32)
            denominator = ((occ_ref[i] + occ_j) - va_block) - vb
            us[i] = (residual / denominator).astype(jnp.bfloat16)
        send_block(us.at[pl.ds(2 * k, 2)], uh.at[p], us_sem, ur_sem, k)
        return c

    lax.fori_loop(0, NI, updates, 0)

    mixing(us)

    def send_mix(t, c):
        k = (r + t) % NI
        for s in range(2):
            i = 2 * k + s
            ms[i] = jnp.transpose(mix[i]).astype(jnp.bfloat16)
            send_mirror(ms.at[i], hm2.at[q], ms_sem, mr_sem.at[q], i)
        return c

    lax.fori_loop(0, NI, send_mix, 0)

    def sums(t, c):
        k = (r + NI - t) % NI
        for s in range(2):
            i = 2 * k + s
            pltpu.make_async_copy(ms.at[0], hm2.at[i], mr_sem.at[i]).wait()
            ws[i] = (mix[i] + hm2[i].astype(jnp.float32)).astype(jnp.bfloat16)
        send_block(ws.at[pl.ds(2 * k, 2)], wh.at[p], ws_sem, wr_sem, k)
        return c

    lax.fori_loop(0, NI, sums, 0)

    pltpu.make_async_copy(uh, uh, ur_sem).wait()
    for s in range(2):
        for place, (ka, kb) in enumerate(PLACES):
            tb[s, ka * B:(ka + 1) * B, kb * B:(kb + 1) * B] = uh[place, s]

    lax.fori_loop(0, 2, inner_half, 0)

    def outer_half(s, c):
        for h in range(2):
            lu[s, h * 256:(h + 1) * 256, :] = outer(s, 2 * h, 2 * h + 2, 0, 4)
        return c

    lax.fori_loop(0, 2, outer_half, 0)

    pltpu.make_async_copy(wh, wh, wr_sem).wait()
    for ka in range(4):
        va_block = jnp.transpose(jnp.broadcast_to(vir_ref[ka:ka + 1, :], (B, B)))
        for kb in range(4):
            place = PLACES.index((ka, kb))
            at = (slice(ka * B, (ka + 1) * B), slice(kb * B, (kb + 1) * B))
            for s in range(2):
                denominator = ((occ_ref[2 * p + s] + occ_j) - va_block) - vir_ref[kb:kb + 1, :]
                residual = 2.0 * lu[(s,) + at] + wh[place, s].astype(jnp.float32)
                out_ref[(s,) + at] = (
                    t0[(s,) + at] + 2.0 * uh[place, s].astype(jnp.float32) + residual / denominator
                )

    pltpu.make_async_copy(most, most, vs_sem).wait()
    rest = pl.ds(0, NI - 1)
    pltpu.make_async_copy(lsl.at[pl.ds(0, 28)], lsl.at[pl.ds(0, 28)], ts_sem).wait()
    pltpu.make_async_copy(lsl.at[pl.ds(0, 28)], lsl.at[pl.ds(0, 28)], ls_sem).wait()
    pltpu.make_async_copy(blk.at[half_places], blk.at[half_places], tfs_sem).wait()
    pltpu.make_async_copy(blk.at[half_places], blk.at[half_places], tgs_sem).wait()
    pltpu.make_async_copy(uh.at[rest], uh.at[rest], us_sem).wait()
    pltpu.make_async_copy(wh.at[rest], wh.at[rest], ws_sem).wait()
    alone = mirror == p

    @pl.when(alone)
    def _():
        left = pl.ds(0, NJ - 1)
        pltpu.make_async_copy(hs.at[left], hs.at[left], hs_sem).wait()
        pltpu.make_async_copy(ms.at[left], ms.at[left], ms_sem).wait()

    @pl.when(jnp.logical_not(alone))
    def _():
        pltpu.make_async_copy(hs, hs, hs_sem).wait()
        pltpu.make_async_copy(ms, ms, ms_sem).wait()


def local(amplitudes, vectors, occupied_fock_block, occ_energy, vir_energy):
    bf, f32 = jnp.bfloat16, jnp.float32
    dma = pltpu.SemaphoreType.DMA
    vmem = pl.BlockSpec(memory_space=pltpu.VMEM)
    out = pl.pallas_call(
        kernel,
        out_shape=pltpu.VMEM((2, 512, 512), f32),
        in_specs=[
            pl.BlockSpec(memory_space=pl.ANY), vmem, vmem,
            pl.BlockSpec(memory_space=pltpu.SMEM), vmem,
        ],
        out_specs=vmem,
        scratch_shapes=[
            pltpu.VMEM((2, 512, 512), f32),
            pltpu.VMEM((2, 512, 512), bf),
            pltpu.VMEM((NI, 2, B, B), bf),
            pltpu.VMEM((3, 16, 2, 16, 512), bf),
            pltpu.VMEM((512, 512), bf),
            pltpu.VMEM((2, 3, 512, 512), bf),
            pltpu.VMEM((NI, 2, B, B), bf),
            pltpu.VMEM((NJ, B, B), bf),
            pltpu.VMEM((2, 8, 2, B, B), bf),
            pltpu.VMEM((NJ, B, B), bf),
            pltpu.VMEM((NJ, B, B), f32),
            pltpu.VMEM((NJ, B, B), bf),
            pltpu.VMEM((NJ, B, B), bf),
            pltpu.VMEM((NJ, B, B), bf),
            pltpu.VMEM((NJ, B, B), bf),
            pltpu.VMEM((NI, 2, B, B), bf),
            pltpu.VMEM((NJ, B, B), bf),
            pltpu.VMEM((NJ, B, B), bf),
            pltpu.VMEM((NJ, B, B), bf),
            pltpu.VMEM((NI, 2, B, B), bf),
            pltpu.VMEM((2, 512, 512), f32),
            dma, dma, dma, dma, dma, dma, dma,
            dma, dma((8,)), dma, dma,
            dma, dma((NI,)), dma, dma((NJ,)),
            dma, dma, dma, dma((NJ,)), dma, dma,
        ],
        compiler_params=pltpu.CompilerParams(
            collective_id=0, has_side_effects=True, vmem_limit_bytes=60 * 1024 * 1024
        ),
        name="doubles",
    )(
        amplitudes.reshape(2, 512, 512), vectors, occupied_fock_block, occ_energy,
        vir_energy.reshape(4, B),
    )
    return out.reshape(2, 1, 512, 512)


def solution(mesh):
    return jax.shard_map(
        local,
        mesh=mesh,
        in_specs=(P("occi", "occj", None, None), P(None, "occj", None), P(), P(), P()),
        out_specs=P("occi", "occj", None, None),
        check_vma=False,
    )
```

```python
import functools

import jax
import jax.numpy as jnp
from jax import lax
from jax.experimental import pallas as pl
from jax.experimental.pallas import tpu as pltpu
from jax.sharding import PartitionSpec as P

MESH = pl.DeviceIdType.MESH
NI, NJ = 16, 32
B = 128
PAIRS = ((0, 1), (0, 2), (0, 3), (1, 2), (1, 3), (2, 3))
PLACES = PAIRS + ((0, 0), (2, 2)) + tuple((b, a) for a, b in PAIRS) + ((1, 1), (3, 3))


def kernel(
    amp_ref, vec_ref, fock_ref, occ_ref, vir_ref, out_ref,
    t0, tb, tfl, vg, kron, inner, blk, tsl, lblk, lsl, mix, hs, hst, hm, us, uh, ms, hm2, ws, wh, lu,
    amp_sem, vs_sem, vr_sem, xs_sem, xr_sem, ts_sem, tr_sem, tfs_sem, tfr_sem, tgs_sem, tgr_sem, ls_sem, lr_sem,
    hs_sem, hr_sem, us_sem, ur_sem, ms_sem, mr_sem, ws_sem, wr_sem,
):
    p = lax.axis_index("occi")
    q = lax.axis_index("occj")
    ylo, z = p // 8, p % 8
    r, core = q // 2, q % 2
    yhi, x = r // 4, r % 4
    y = 2 * yhi + ylo
    other = 2 * r + 1 - core
    flip = (p + 8) % NI
    ours, theirs = 8 * ylo, 8 * (1 - ylo)
    mirror = (p + 8 * (1 - z // 6)) % NI

    load = pltpu.make_async_copy(amp_ref, t0, amp_sem)
    load.start()

    barrier = pltpu.get_barrier_semaphore()

    def greet(dev):
        pl.semaphore_signal(barrier, inc=1, device_id=dev, device_id_type=MESH)

    def greet_column(t, c):
        greet(((p + t) % NI, q))
        return c

    def at_y(ny, nx):
        return ((ny % 2) * 8 + z, ((ny // 2) * 4 + nx) * 2 + core)

    def greet_mirror(i, c):
        @pl.when(jnp.logical_not((mirror == p) & (i == q)))
        def _():
            greet((mirror, i))

        return c

    def greet_vec_near(t, c):
        greet(at_y(y, (x + t) % 4))
        return c

    def greet_vec_far(t, c):
        d = 1 + t // 4
        up = (d + y) % 2
        greet(at_y((y - d * up + d * (1 - up) + 8) % 8, (x + t) % 4))
        return c

    greet((p, other))
    lax.fori_loop(1, NI, greet_column, 0)
    lax.fori_loop(1, 4, greet_vec_near, 0)
    lax.fori_loop(0, 12, greet_vec_far, 0)
    lax.fori_loop(0, NJ, greet_mirror, 0)

    rows = lax.broadcasted_iota(jnp.int32, (512, NJ), 0) // 16
    cols = lax.broadcasted_iota(jnp.int32, (512, NJ), 1)
    spread = (rows == cols).astype(jnp.float32).astype(jnp.bfloat16)
    wide = lax.dot_general(
        fock_ref[...], spread, (((0,), (1,)), ((), ())), preferred_element_type=jnp.float32
    ).astype(jnp.bfloat16)
    tall = jnp.dot(spread, wide, preferred_element_type=jnp.float32)
    same = (
        lax.broadcasted_iota(jnp.int32, (512, 512), 0) % 16
        == lax.broadcasted_iota(jnp.int32, (512, 512), 1) % 16
    )
    kron[...] = jnp.where(same, -tall, 0.0).astype(jnp.bfloat16)

    load.wait()
    for s in range(2):
        for place, (ka, kb) in enumerate(PLACES):
            part = t0[s, ka * B:(ka + 1) * B, kb * B:(kb + 1) * B].astype(jnp.bfloat16)
            blk[place, s] = part
            tb[s, ka * B:(ka + 1) * B, kb * B:(kb + 1) * B] = part

    pl.semaphore_wait(barrier, 1 + NI - 1 + 15 + NJ - z // 6)

    vg[:, r, core] = vec_ref[...]
    sign = 2 * ylo - 1

    def send_vec(ty, tx):
        pltpu.make_async_remote_copy(
            vec_ref, vg.at[:, r, core], vs_sem, vr_sem,
            device_id=at_y((y + sign * ty + 8) % 8, (x + tx) % 4), device_id_type=MESH,
        ).start()

    def send_vec_far(t, c):
        send_vec(1 + t // 4, t % 4)
        return c

    def send_vec_near(t, c):
        send_vec(0, t)
        return c

    def send_block(src, dst, send, recv, k):
        @pl.when(k != p)
        def _():
            pltpu.make_async_remote_copy(
                src, dst, send, recv, device_id=(k, q), device_id_type=MESH
            ).start()

        @pl.when(k == p)
        def _():
            pltpu.make_async_copy(src, dst, recv).start()

    def cross_t(t, c):
        place = theirs + around(t)
        pltpu.make_async_remote_copy(
            blk.at[place], tfl.at[place], tfs_sem, tfr_sem.at[place - theirs],
            device_id=(flip, q), device_id_type=MESH,
        ).start()
        return c

    def around(t):
        return (z + ((t + 1) // 2) * (2 * (t % 2) - 1) + 8) % 8

    def send_t(t, c):
        k = ours + around(t)
        send_block(blk.at[k], tsl.at[pl.ds(2 * p, 2)], ts_sem, tr_sem, k)
        return c

    def pass_t(t, c):
        zk = around(t)
        pltpu.make_async_copy(blk.at[0], tfl.at[ours + zk], tfr_sem.at[zk]).wait()
        send_block(tfl.at[ours + zk], tsl.at[pl.ds(2 * flip, 2)], ts_sem, tr_sem, ours + zk)
        return c

    lax.fori_loop(0, 8, cross_t, 0)
    lax.fori_loop(0, 8, send_t, 0)
    lax.fori_loop(0, 12, send_vec_far, 0)
    lax.fori_loop(1, 4, send_vec_near, 0)
    lax.fori_loop(0, 8, pass_t, 0)
    pltpu.make_async_remote_copy(
        blk.at[pl.ds(ours, 8)], tfl.at[pl.ds(ours, 8)], tgs_sem, tgr_sem,
        device_id=(flip, q), device_id_type=MESH,
    ).start()

    most = vg.at[:, pl.ds(0, 15), 0]
    pltpu.make_async_copy(most, most, vr_sem).wait()
    swap = pltpu.make_async_remote_copy(
        vg.at[:, :, core], vg.at[:, :, core], xs_sem, xr_sem,
        device_id=(p, other), device_id_type=MESH,
    )
    swap.start()
    swap.wait_send()
    pltpu.make_async_copy(vg.at[:, :, 0], vg.at[:, :, 0], xr_sem).wait()

    def turn_of(t):
        return t // 2 + 4 * (t % 2)

    def inner_half(s, c):
        for h in range(2):
            piece = tb[s, h * 256:(h + 1) * 256, :]
            for l in range(3):
                inner[s, l, h * 256:(h + 1) * 256, :] = lax.dot_general(
                    piece, vg[l].reshape(512, 512), (((1,), (1,)), ((), ())),
                    preferred_element_type=jnp.float32,
                ).astype(jnp.bfloat16)
        return c

    def outer(s, first, last, left, right):
        total = None
        for l in range(3):
            term = jnp.dot(
                vg[l, first * 4:last * 4].reshape((last - first) * B, 512),
                inner[s, l, :, left * B:right * B], preferred_element_type=jnp.float32,
            )
            total = term if total is None else total + term
        return total

    def ladder_blocks(turn):
        lax.fori_loop(0, 2, inner_half, 0)
        for plane, parts in enumerate((((0, 1, 0, 4), (1, 3, 2, 4)), ((3, 4, 0, 4), (1, 3, 0, 2)))):
            def one_pair(s, c, parts=parts, plane=plane):
                for first, last, left, right in parts:
                    total = outer(s, first, last, left, right)
                    for ka in range(first, last):
                        for kb in range(left, right):
                            zk = PLACES.index((ka, kb)) - 8 * plane
                            lblk[turn, zk, s] = total[
                                (ka - first) * B:(ka - first + 1) * B, (kb - left) * B:(kb - left + 1) * B
                            ].astype(jnp.bfloat16)
                return c

            @pl.when(ylo == plane)
            def _():
                lax.fori_loop(0, 2, one_pair, 0)

        origin = (p, flip)[turn]

        def send_l(t, c):
            zk = (z + 3 * NI - r - turn_of(t)) % 8
            send_block(
                lblk.at[turn, zk], lsl.at[pl.ds(2 * origin, 2)], ls_sem, lr_sem.at[origin], ours + zk
            )
            return c

        lax.fori_loop(0, 8, send_l, 0)

    ladder_blocks(0)

    def mixing(source):
        def group(g, c):
            lines = [pl.ds(pl.multiple_of(g * 32 + 16 * h, 16), 16) for h in range(2)]
            pieces = [source[:, at, :].reshape(512, B) for at in lines]
            got = jnp.dot(
                kron[...], jnp.concatenate(pieces, axis=1), preferred_element_type=jnp.float32
            )
            for h in range(2):
                mix[:, lines[h], :] = got[:, h * B:(h + 1) * B].reshape(NJ, 16, B)
            return c

        lax.fori_loop(0, B // 32, group, 0)

    pltpu.make_async_copy(tsl, tsl, tr_sem).wait()
    mixing(tsl)

    half_places = pl.ds(0, 8)
    pltpu.make_async_copy(blk.at[half_places], blk.at[half_places], tgr_sem).wait()
    for s in range(2):
        for place, (ka, kb) in enumerate(PLACES):
            tb[s, ka * B:(ka + 1) * B, kb * B:(kb + 1) * B] = tfl[place, s]
    ladder_blocks(1)

    def send_mirror(src, dst, send, recv, i):
        alone = (mirror == p) & (i == q)

        @pl.when(jnp.logical_not(alone))
        def _():
            pltpu.make_async_remote_copy(
                src, dst, send, recv, device_id=(mirror, i), device_id_type=MESH
            ).start()

        @pl.when(alone)
        def _():
            pltpu.make_async_copy(src, dst, recv).start()

    def halves(t, c):
        k = ((ylo + t // 8) % 2) * 8 + (z + r + turn_of(t % 8)) % 8
        pltpu.make_async_copy(lblk.at[0, 0], lsl.at[pl.ds(2 * k, 2)], lr_sem.at[k]).wait()
        for s in range(2):
            i = 2 * k + s
            half = (mix[i] + lsl[i].astype(jnp.float32)).astype(jnp.bfloat16).astype(jnp.float32)
            hst[i] = jnp.transpose(half).astype(jnp.bfloat16)
            send_mirror(hst.at[i], hm.at[q], hs_sem, hr_sem.at[q], i)
            hs[i] = half.astype(jnp.bfloat16)
        return c

    lax.fori_loop(0, NI, halves, 0)

    va = jnp.zeros((1, B), jnp.float32)
    vb = jnp.zeros((1, B), jnp.float32)
    for place, (ka, kb) in enumerate(PLACES):
        here = p == place
        va = jnp.where(here, vir_ref[ka:ka + 1, :], va)
        vb = jnp.where(here, vir_ref[kb:kb + 1, :], vb)
    va_block = jnp.transpose(jnp.broadcast_to(va, (B, B)))
    occ_j = occ_ref[q]

    def updates(t, c):
        k = ((r // 8 + t) % 2) * 8 + (r + 2 * NI - z - turn_of(t // 2)) % 8
        for s in range(2):
            i = 2 * k + s
            pltpu.make_async_copy(hs.at[0], hm.at[i], hr_sem.at[i]).wait()
            residual = hs[i].astype(jnp.float32) + hm[i].astype(jnp.float32)
            denominator = ((occ_ref[i] + occ_j) - va_block) - vb
            us[i] = (residual / denominator).astype(jnp.bfloat16)
        send_block(us.at[pl.ds(2 * k, 2)], uh.at[p], us_sem, ur_sem, k)
        return c

    lax.fori_loop(0, NI, updates, 0)

    mixing(us)

    def send_mix(t, c):
        k = ((yhi + z // 4 + 2 * (mirror // 8) + t) % 4) * 4 + (x + z + t // 4) % 4
        for s in range(2):
            i = 2 * k + s
            ms[i] = jnp.transpose(mix[i]).astype(jnp.bfloat16)
            send_mirror(ms.at[i], hm2.at[q], ms_sem, mr_sem.at[q], i)
        return c

    lax.fori_loop(0, NI, send_mix, 0)

    def sums(t, c):
        k = ((yhi + 24 - z // 4 - 2 * ylo - t) % 4) * 4 + (x + 16 - z - t // 4) % 4
        for s in range(2):
            i = 2 * k + s
            pltpu.make_async_copy(ms.at[0], hm2.at[i], mr_sem.at[i]).wait()
            ws[i] = (mix[i] + hm2[i].astype(jnp.float32)).astype(jnp.bfloat16)
        send_block(ws.at[pl.ds(2 * k, 2)], wh.at[p], ws_sem, wr_sem, k)
        return c

    lax.fori_loop(0, NI, sums, 0)

    pltpu.make_async_copy(uh, uh, ur_sem).wait()
    for s in range(2):
        for place, (ka, kb) in enumerate(PLACES):
            tb[s, ka * B:(ka + 1) * B, kb * B:(kb + 1) * B] = uh[place, s]

    lax.fori_loop(0, 2, inner_half, 0)

    def outer_half(s, c):
        for h in range(2):
            lu[s, h * 256:(h + 1) * 256, :] = outer(s, 2 * h, 2 * h + 2, 0, 4)
        return c

    lax.fori_loop(0, 2, outer_half, 0)

    pltpu.make_async_copy(wh, wh, wr_sem).wait()
    for ka in range(4):
        va_block = jnp.transpose(jnp.broadcast_to(vir_ref[ka:ka + 1, :], (B, B)))
        for kb in range(4):
            place = PLACES.index((ka, kb))
            at = (slice(ka * B, (ka + 1) * B), slice(kb * B, (kb + 1) * B))
            for s in range(2):
                denominator = ((occ_ref[2 * p + s] + occ_j) - va_block) - vir_ref[kb:kb + 1, :]
                residual = 2.0 * lu[(s,) + at] + wh[place, s].astype(jnp.float32)
                out_ref[(s,) + at] = (
                    t0[(s,) + at] + 2.0 * uh[place, s].astype(jnp.float32) + residual / denominator
                )

    pltpu.make_async_copy(most, most, vs_sem).wait()
    rest = pl.ds(0, NI - 1)
    pltpu.make_async_copy(lsl.at[pl.ds(0, 28)], lsl.at[pl.ds(0, 28)], ts_sem).wait()
    pltpu.make_async_copy(lsl.at[pl.ds(0, 28)], lsl.at[pl.ds(0, 28)], ls_sem).wait()
    pltpu.make_async_copy(blk.at[half_places], blk.at[half_places], tfs_sem).wait()
    pltpu.make_async_copy(blk.at[half_places], blk.at[half_places], tgs_sem).wait()
    pltpu.make_async_copy(uh.at[rest], uh.at[rest], us_sem).wait()
    pltpu.make_async_copy(wh.at[rest], wh.at[rest], ws_sem).wait()
    alone = mirror == p

    @pl.when(alone)
    def _():
        left = pl.ds(0, NJ - 1)
        pltpu.make_async_copy(hs.at[left], hs.at[left], hs_sem).wait()
        pltpu.make_async_copy(ms.at[left], ms.at[left], ms_sem).wait()

    @pl.when(jnp.logical_not(alone))
    def _():
        pltpu.make_async_copy(hs, hs, hs_sem).wait()
        pltpu.make_async_copy(ms, ms, ms_sem).wait()


def local(amplitudes, vectors, occupied_fock_block, occ_energy, vir_energy):
    bf, f32 = jnp.bfloat16, jnp.float32
    dma = pltpu.SemaphoreType.DMA
    vmem = pl.BlockSpec(memory_space=pltpu.VMEM)
    out = pl.pallas_call(
        kernel,
        out_shape=pltpu.VMEM((2, 512, 512), f32),
        in_specs=[
            pl.BlockSpec(memory_space=pl.ANY), vmem, vmem,
            pl.BlockSpec(memory_space=pltpu.SMEM), vmem,
        ],
        out_specs=vmem,
        scratch_shapes=[
            pltpu.VMEM((2, 512, 512), f32),
            pltpu.VMEM((2, 512, 512), bf),
            pltpu.VMEM((NI, 2, B, B), bf),
            pltpu.VMEM((3, 16, 2, 16, 512), bf),
            pltpu.VMEM((512, 512), bf),
            pltpu.VMEM((2, 3, 512, 512), bf),
            pltpu.VMEM((NI, 2, B, B), bf),
            pltpu.VMEM((NJ, B, B), bf),
            pltpu.VMEM((2, 8, 2, B, B), bf),
            pltpu.VMEM((NJ, B, B), bf),
            pltpu.VMEM((NJ, B, B), f32),
            pltpu.VMEM((NJ, B, B), bf),
            pltpu.VMEM((NJ, B, B), bf),
            pltpu.VMEM((NJ, B, B), bf),
            pltpu.VMEM((NJ, B, B), bf),
            pltpu.VMEM((NI, 2, B, B), bf),
            pltpu.VMEM((NJ, B, B), bf),
            pltpu.VMEM((NJ, B, B), bf),
            pltpu.VMEM((NJ, B, B), bf),
            pltpu.VMEM((NI, 2, B, B), bf),
            pltpu.VMEM((2, 512, 512), f32),
            dma, dma, dma, dma, dma, dma, dma,
            dma, dma((8,)), dma, dma,
            dma, dma((NI,)), dma, dma((NJ,)),
            dma, dma, dma, dma((NJ,)), dma, dma,
        ],
        compiler_params=pltpu.CompilerParams(
            collective_id=0, has_side_effects=True, vmem_limit_bytes=60 * 1024 * 1024
        ),
        name="doubles",
    )(
        amplitudes.reshape(2, 512, 512), vectors, occupied_fock_block, occ_energy,
        vir_energy.reshape(4, B),
    )
    return out.reshape(2, 1, 512, 512)


def solution(mesh):
    return jax.shard_map(
        local,
        mesh=mesh,
        in_specs=(P("occi", "occj", None, None), P(None, "occj", None), P(), P(), P()),
        out_specs=P("occi", "occj", None, None),
        check_vma=False,
    )
```

```python
import functools

import jax
import jax.numpy as jnp
from jax import lax
from jax.experimental import pallas as pl
from jax.experimental.pallas import tpu as pltpu
from jax.sharding import PartitionSpec as P

MESH = pl.DeviceIdType.MESH
NI, NJ = 16, 32
B = 128
PAIRS = ((0, 1), (0, 2), (0, 3), (1, 2), (1, 3), (2, 3))
PLACES = PAIRS + ((0, 0), (2, 2)) + tuple((b, a) for a, b in PAIRS) + ((1, 1), (3, 3))


def kernel(
    amp_ref, vec_ref, fock_ref, occ_ref, vir_ref, out_ref,
    t0, tb, tfl, vg, kron, inner, blk, tsl, lblk, lsl, mix, hs, hst, hm, us, uh, ms, hm2, ws, wh, lu,
    amp_sem, vs_sem, vr_sem, xs_sem, xr_sem, ts_sem, tr_sem, tfs_sem, tfr_sem, tgs_sem, tgr_sem, ls_sem, lr_sem,
    hs_sem, hr_sem, us_sem, ur_sem, ms_sem, mr_sem, ws_sem, wr_sem,
):
    p = lax.axis_index("occi")
    q = lax.axis_index("occj")
    ylo, z = p // 8, p % 8
    r, core = q // 2, q % 2
    yhi, x = r // 4, r % 4
    y = 2 * yhi + ylo
    other = 2 * r + 1 - core
    flip = (p + 8) % NI
    ours, theirs = 8 * ylo, 8 * (1 - ylo)
    mirror = (p + 8 * (1 - z // 6)) % NI

    load = pltpu.make_async_copy(amp_ref, t0, amp_sem)
    load.start()

    barrier = pltpu.get_barrier_semaphore()

    def greet(dev):
        pl.semaphore_signal(barrier, inc=1, device_id=dev, device_id_type=MESH)

    def greet_column(t, c):
        greet(((p + t) % NI, q))
        return c

    def at_y(ny, nx):
        return ((ny % 2) * 8 + z, ((ny // 2) * 4 + nx) * 2 + core)

    def greet_mirror(i, c):
        @pl.when(jnp.logical_not((mirror == p) & (i == q)))
        def _():
            greet((mirror, i))

        return c

    def greet_vec_near(t, c):
        greet(at_y(y, (x + t) % 4))
        return c

    def greet_vec_far(t, c):
        d = 1 + t // 4
        up = (d + y) % 2
        greet(at_y((y - d * up + d * (1 - up) + 8) % 8, (x + t) % 4))
        return c

    greet((p, other))
    lax.fori_loop(1, NI, greet_column, 0)
    lax.fori_loop(1, 4, greet_vec_near, 0)
    lax.fori_loop(0, 12, greet_vec_far, 0)
    lax.fori_loop(0, NJ, greet_mirror, 0)

    rows = lax.broadcasted_iota(jnp.int32, (512, NJ), 0) // 16
    cols = lax.broadcasted_iota(jnp.int32, (512, NJ), 1)
    spread = (rows == cols).astype(jnp.float32).astype(jnp.bfloat16)
    wide = lax.dot_general(
        fock_ref[...], spread, (((0,), (1,)), ((), ())), preferred_element_type=jnp.float32
    ).astype(jnp.bfloat16)
    tall = jnp.dot(spread, wide, preferred_element_type=jnp.float32)
    same = (
        lax.broadcasted_iota(jnp.int32, (512, 512), 0) % 16
        == lax.broadcasted_iota(jnp.int32, (512, 512), 1) % 16
    )
    kron[...] = jnp.where(same, -tall, 0.0).astype(jnp.bfloat16)

    load.wait()
    for s in range(2):
        for place, (ka, kb) in enumerate(PLACES):
            part = t0[s, ka * B:(ka + 1) * B, kb * B:(kb + 1) * B].astype(jnp.bfloat16)
            blk[place, s] = part
            tb[s, ka * B:(ka + 1) * B, kb * B:(kb + 1) * B] = part

    pl.semaphore_wait(barrier, 1 + NI - 1 + 15 + NJ - z // 6)

    vg[:, r, core] = vec_ref[...]
    sign = 2 * ylo - 1

    def send_vec(ty, tx):
        pltpu.make_async_remote_copy(
            vec_ref, vg.at[:, r, core], vs_sem, vr_sem,
            device_id=at_y((y + sign * ty + 8) % 8, (x + tx) % 4), device_id_type=MESH,
        ).start()

    def send_vec_far(t, c):
        send_vec(1 + t // 4, t % 4)
        return c

    def send_vec_near(t, c):
        send_vec(0, t)
        return c

    def send_block(src, dst, send, recv, k):
        @pl.when(k != p)
        def _():
            pltpu.make_async_remote_copy(
                src, dst, send, recv, device_id=(k, q), device_id_type=MESH
            ).start()

        @pl.when(k == p)
        def _():
            pltpu.make_async_copy(src, dst, recv).start()

    def cross_t(t, c):
        place = theirs + around(t)
        pltpu.make_async_remote_copy(
            blk.at[place], tfl.at[place], tfs_sem, tfr_sem.at[place - theirs],
            device_id=(flip, q), device_id_type=MESH,
        ).start()
        return c

    def around(t):
        return (z + ((t + 1) // 2) * (2 * (t % 2) - 1) + 8) % 8

    def send_t(t, c):
        k = ours + around(t)
        send_block(blk.at[k], tsl.at[pl.ds(2 * p, 2)], ts_sem, tr_sem, k)
        return c

    def pass_t(t, c):
        zk = around(t)
        pltpu.make_async_copy(blk.at[0], tfl.at[ours + zk], tfr_sem.at[zk]).wait()
        send_block(tfl.at[ours + zk], tsl.at[pl.ds(2 * flip, 2)], ts_sem, tr_sem, ours + zk)
        return c

    lax.fori_loop(0, 8, cross_t, 0)
    lax.fori_loop(0, 8, send_t, 0)
    lax.fori_loop(0, 12, send_vec_far, 0)
    lax.fori_loop(1, 4, send_vec_near, 0)
    lax.fori_loop(0, 8, pass_t, 0)
    pltpu.make_async_remote_copy(
        blk.at[pl.ds(ours, 8)], tfl.at[pl.ds(ours, 8)], tgs_sem, tgr_sem,
        device_id=(flip, q), device_id_type=MESH,
    ).start()

    most = vg.at[:, pl.ds(0, 15), 0]
    pltpu.make_async_copy(most, most, vr_sem).wait()
    swap = pltpu.make_async_remote_copy(
        vg.at[:, :, core], vg.at[:, :, core], xs_sem, xr_sem,
        device_id=(p, other), device_id_type=MESH,
    )
    swap.start()
    swap.wait_send()
    pltpu.make_async_copy(vg.at[:, :, 0], vg.at[:, :, 0], xr_sem).wait()

    def turn_of(t):
        return t // 2 + 4 * (t % 2)

    def inner_half(s, c):
        for h in range(2):
            piece = tb[s, h * 256:(h + 1) * 256, :]
            for l in range(3):
                inner[s, l, h * 256:(h + 1) * 256, :] = lax.dot_general(
                    piece, vg[l].reshape(512, 512), (((1,), (1,)), ((), ())),
                    preferred_element_type=jnp.float32,
                ).astype(jnp.bfloat16)
        return c

    def outer(s, first, last, left, right):
        total = None
        for l in range(3):
            term = jnp.dot(
                vg[l, first * 4:last * 4].reshape((last - first) * B, 512),
                inner[s, l, :, left * B:right * B], preferred_element_type=jnp.float32,
            )
            total = term if total is None else total + term
        return total

    def ladder_blocks(turn):
        lax.fori_loop(0, 2, inner_half, 0)
        for plane, parts in enumerate((((0, 1, 0, 4), (1, 3, 2, 4)), ((3, 4, 0, 4), (1, 3, 0, 2)))):
            def one_pair(s, c, parts=parts, plane=plane):
                for first, last, left, right in parts:
                    total = outer(s, first, last, left, right)
                    for ka in range(first, last):
                        for kb in range(left, right):
                            zk = PLACES.index((ka, kb)) - 8 * plane
                            lblk[turn, zk, s] = total[
                                (ka - first) * B:(ka - first + 1) * B, (kb - left) * B:(kb - left + 1) * B
                            ].astype(jnp.bfloat16)
                return c

            @pl.when(ylo == plane)
            def _():
                lax.fori_loop(0, 2, one_pair, 0)

        origin = (p, flip)[turn]

        def send_l(t, c):
            zk = (z + 3 * NI - r - turn_of(t)) % 8
            send_block(
                lblk.at[turn, zk], lsl.at[pl.ds(2 * origin, 2)], ls_sem, lr_sem.at[origin], ours + zk
            )
            return c

        lax.fori_loop(0, 8, send_l, 0)

    ladder_blocks(0)

    def mixing(source):
        def group(g, c):
            lines = [pl.ds(pl.multiple_of(g * 32 + 16 * h, 16), 16) for h in range(2)]
            pieces = [source[:, at, :].reshape(512, B) for at in lines]
            got = jnp.dot(
                kron[...], jnp.concatenate(pieces, axis=1), preferred_element_type=jnp.float32
            )
            for h in range(2):
                mix[:, lines[h], :] = got[:, h * B:(h + 1) * B].reshape(NJ, 16, B)
            return c

        lax.fori_loop(0, B // 32, group, 0)

    pltpu.make_async_copy(tsl, tsl, tr_sem).wait()
    mixing(tsl)

    half_places = pl.ds(0, 8)
    pltpu.make_async_copy(blk.at[half_places], blk.at[half_places], tgr_sem).wait()
    for s in range(2):
        for place, (ka, kb) in enumerate(PLACES):
            tb[s, ka * B:(ka + 1) * B, kb * B:(kb + 1) * B] = tfl[place, s]
    ladder_blocks(1)

    def send_mirror(src, dst, send, recv, i):
        alone = (mirror == p) & (i == q)

        @pl.when(jnp.logical_not(alone))
        def _():
            pltpu.make_async_remote_copy(
                src, dst, send, recv, device_id=(mirror, i), device_id_type=MESH
            ).start()

        @pl.when(alone)
        def _():
            pltpu.make_async_copy(src, dst, recv).start()

    def halves(t, c):
        k = ((ylo + t // 8) % 2) * 8 + (z + r + turn_of(t % 8)) % 8
        pltpu.make_async_copy(lblk.at[0, 0], lsl.at[pl.ds(2 * k, 2)], lr_sem.at[k]).wait()
        for s in range(2):
            i = 2 * k + s
            half = (mix[i] + lsl[i].astype(jnp.float32)).astype(jnp.bfloat16).astype(jnp.float32)
            hst[i] = jnp.transpose(half).astype(jnp.bfloat16)
            send_mirror(hst.at[i], hm.at[q], hs_sem, hr_sem.at[q], i)
            hs[i] = half.astype(jnp.bfloat16)
        return c

    lax.fori_loop(0, NI, halves, 0)

    va = jnp.zeros((1, B), jnp.float32)
    vb = jnp.zeros((1, B), jnp.float32)
    for place, (ka, kb) in enumerate(PLACES):
        here = p == place
        va = jnp.where(here, vir_ref[ka:ka + 1, :], va)
        vb = jnp.where(here, vir_ref[kb:kb + 1, :], vb)
    va_block = jnp.transpose(jnp.broadcast_to(va, (B, B)))
    occ_j = occ_ref[q]

    def updates(t, c):
        k = ((r // 8 + t) % 2) * 8 + (r + 2 * NI - z - turn_of(t // 2)) % 8
        for s in range(2):
            i = 2 * k + s
            pltpu.make_async_copy(hs.at[0], hm.at[i], hr_sem.at[i]).wait()
            residual = hs[i].astype(jnp.float32) + hm[i].astype(jnp.float32)
            denominator = ((occ_ref[i] + occ_j) - va_block) - vb
            us[i] = (residual / denominator).astype(jnp.bfloat16)
        send_block(us.at[pl.ds(2 * k, 2)], uh.at[p], us_sem, ur_sem, k)
        return c

    lax.fori_loop(0, NI, updates, 0)

    mixing(us)

    def send_mix(t, c):
        k = ((yhi + z // 4 + 2 * (mirror // 8) + t) % 4) * 4 + (x + z + t // 4) % 4
        for s in range(2):
            i = 2 * k + s
            ms[i] = jnp.transpose(mix[i]).astype(jnp.bfloat16)
            send_mirror(ms.at[i], hm2.at[q], ms_sem, mr_sem.at[q], i)
        return c

    lax.fori_loop(0, NI, send_mix, 0)

    def sums(t, c):
        k = ((yhi + 24 - z // 4 - 2 * ylo - t) % 4) * 4 + (x + 16 - z - t // 4) % 4
        for s in range(2):
            i = 2 * k + s
            pltpu.make_async_copy(ms.at[0], hm2.at[i], mr_sem.at[i]).wait()
            ws[i] = (mix[i] + hm2[i].astype(jnp.float32)).astype(jnp.bfloat16)
        send_block(ws.at[pl.ds(2 * k, 2)], wh.at[p], ws_sem, wr_sem, k)
        return c

    lax.fori_loop(0, NI, sums, 0)

    pltpu.make_async_copy(uh, uh, ur_sem).wait()
    for s in range(2):
        for place, (ka, kb) in enumerate(PLACES):
            tb[s, ka * B:(ka + 1) * B, kb * B:(kb + 1) * B] = uh[place, s]

    lax.fori_loop(0, 2, inner_half, 0)

    def outer_half(s, c):
        for h in range(2):
            lu[s, h * 256:(h + 1) * 256, :] = outer(s, 2 * h, 2 * h + 2, 0, 4)
        return c

    lax.fori_loop(0, 2, outer_half, 0)

    for ka in range(4):
        va_block = jnp.transpose(jnp.broadcast_to(vir_ref[ka:ka + 1, :], (B, B)))
        for kb in range(4):
            place = PLACES.index((ka, kb))
            at = (slice(ka * B, (ka + 1) * B), slice(kb * B, (kb + 1) * B))
            for s in range(2):
                inverse = 1.0 / (((occ_ref[2 * p + s] + occ_j) - va_block) - vir_ref[kb:kb + 1, :])
                lu[(s,) + at] = (
                    t0[(s,) + at] + 2.0 * uh[place, s].astype(jnp.float32)
                    + 2.0 * lu[(s,) + at] * inverse
                )
                t0[(s,) + at] = inverse

    pltpu.make_async_copy(wh, wh, wr_sem).wait()
    for place, (ka, kb) in enumerate(PLACES):
        at = (slice(ka * B, (ka + 1) * B), slice(kb * B, (kb + 1) * B))
        for s in range(2):
            out_ref[(s,) + at] = lu[(s,) + at] + wh[place, s].astype(jnp.float32) * t0[(s,) + at]

    pltpu.make_async_copy(most, most, vs_sem).wait()
    rest = pl.ds(0, NI - 1)
    pltpu.make_async_copy(lsl.at[pl.ds(0, 28)], lsl.at[pl.ds(0, 28)], ts_sem).wait()
    pltpu.make_async_copy(lsl.at[pl.ds(0, 28)], lsl.at[pl.ds(0, 28)], ls_sem).wait()
    pltpu.make_async_copy(blk.at[half_places], blk.at[half_places], tfs_sem).wait()
    pltpu.make_async_copy(blk.at[half_places], blk.at[half_places], tgs_sem).wait()
    pltpu.make_async_copy(uh.at[rest], uh.at[rest], us_sem).wait()
    pltpu.make_async_copy(wh.at[rest], wh.at[rest], ws_sem).wait()
    alone = mirror == p

    @pl.when(alone)
    def _():
        left = pl.ds(0, NJ - 1)
        pltpu.make_async_copy(hs.at[left], hs.at[left], hs_sem).wait()
        pltpu.make_async_copy(ms.at[left], ms.at[left], ms_sem).wait()

    @pl.when(jnp.logical_not(alone))
    def _():
        pltpu.make_async_copy(hs, hs, hs_sem).wait()
        pltpu.make_async_copy(ms, ms, ms_sem).wait()


def local(amplitudes, vectors, occupied_fock_block, occ_energy, vir_energy):
    bf, f32 = jnp.bfloat16, jnp.float32
    dma = pltpu.SemaphoreType.DMA
    vmem = pl.BlockSpec(memory_space=pltpu.VMEM)
    out = pl.pallas_call(
        kernel,
        out_shape=pltpu.VMEM((2, 512, 512), f32),
        in_specs=[
            pl.BlockSpec(memory_space=pl.ANY), vmem, vmem,
            pl.BlockSpec(memory_space=pltpu.SMEM), vmem,
        ],
        out_specs=vmem,
        scratch_shapes=[
            pltpu.VMEM((2, 512, 512), f32),
            pltpu.VMEM((2, 512, 512), bf),
            pltpu.VMEM((NI, 2, B, B), bf),
            pltpu.VMEM((3, 16, 2, 16, 512), bf),
            pltpu.VMEM((512, 512), bf),
            pltpu.VMEM((2, 3, 512, 512), bf),
            pltpu.VMEM((NI, 2, B, B), bf),
            pltpu.VMEM((NJ, B, B), bf),
            pltpu.VMEM((2, 8, 2, B, B), bf),
            pltpu.VMEM((NJ, B, B), bf),
            pltpu.VMEM((NJ, B, B), f32),
            pltpu.VMEM((NJ, B, B), bf),
            pltpu.VMEM((NJ, B, B), bf),
            pltpu.VMEM((NJ, B, B), bf),
            pltpu.VMEM((NJ, B, B), bf),
            pltpu.VMEM((NI, 2, B, B), bf),
            pltpu.VMEM((NJ, B, B), bf),
            pltpu.VMEM((NJ, B, B), bf),
            pltpu.VMEM((NJ, B, B), bf),
            pltpu.VMEM((NI, 2, B, B), bf),
            pltpu.VMEM((2, 512, 512), f32),
            dma, dma, dma, dma, dma, dma, dma,
            dma, dma((8,)), dma, dma,
            dma, dma((NI,)), dma, dma((NJ,)),
            dma, dma, dma, dma((NJ,)), dma, dma,
        ],
        compiler_params=pltpu.CompilerParams(
            collective_id=0, has_side_effects=True, vmem_limit_bytes=60 * 1024 * 1024
        ),
        name="doubles",
    )(
        amplitudes.reshape(2, 512, 512), vectors, occupied_fock_block, occ_energy,
        vir_energy.reshape(4, B),
    )
    return out.reshape(2, 1, 512, 512)


def solution(mesh):
    return jax.shard_map(
        local,
        mesh=mesh,
        in_specs=(P("occi", "occj", None, None), P(None, "occj", None), P(), P(), P()),
        out_specs=P("occi", "occj", None, None),
        check_vma=False,
    )
```
